32 devices in a mesh: layer: 8 (over z, core), space: 4 (over y, x).
Axes of the slice: x: 2, y: 2, z: 4, core: 2. Of those that a mesh axis runs over, the one named last changes fastest.
Arguments:
- initial: float32 [32, 4, 1024], P(None, 'space'), may hold values from -6 to 6
- kernels: bfloat16 [16, 27, 32, 32], P('layer'), may hold values from -0.21875 to 0.21875
- biases: float32 [16, 32], P('layer'), may hold values from -3 to 3
Outputs:
- states: float32 [16, 32, 4, 1024], P('layer', None, 'space')
The draws below stay inside these ranges and needn't reach their ends.
All inputs are finite; a program needn't handle non-finite values.
Results may differ from the reference program's by a relative error of at most 0.0041.
Values may be sent and summed in bfloat16 or wider, within the bound.
A program may use at most 64 MiB of HBM per device.

```python
import jax
import jax.numpy as jnp
from jax import lax

C = 32
NY = 16
NZ = 64
LEVELS = 3
CYCLES = 2
BLOCKS = 16
NX = 4


def steps_of(stream_key, extent, pieces, least, high):
    level, own = 1.0, jax.random.fold_in(stream_key, 6)
    for position, blocks in pieces:
        steps = jnp.exp(jax.random.uniform(jax.random.fold_in(own, position), (blocks,), jnp.float32, least / len(pieces), high / len(pieces)))
        level = level * jnp.repeat(steps, extent[position] // blocks).reshape([-1 if axis == position else 1 for axis in range(len(extent))])
    return level


def bell_draw(key, dims, scale, most, shards=(), held_as=jnp.bfloat16):
    array = scale * jax.random.normal(key, dims, jnp.float32)
    if shards:
        array = array * steps_of(key, dims, shards, -0.22, 0.18)
    return jnp.clip(array, -most, most).astype(held_as)


def setup_inputs(seed: int = 0) -> dict:
    key_list = jax.random.split(jax.random.key(seed), 4)
    return {
        "initial": bell_draw(key_list[0], (C, NX, NY * NZ), 1.0, 6.0, ((1, 4),), jnp.float32),
        "kernels": bell_draw(key_list[1], (BLOCKS, 27, C, C), (27 * C) ** -0.5, 0.21875, ((0, 8),)),
        "biases": bell_draw(key_list[2], (BLOCKS, C), 0.5, 3.0, ((0, 8),), jnp.float32),
    }


step_base = 0.125


def advance(values, kernel_one, bias_one, step_size):
    volume = values.astype(jnp.bfloat16).reshape(1, C, NX, NY, NZ)
    weight = kernel_one.reshape(3, 3, 3, C, C).transpose(3, 4, 0, 1, 2)
    convolved = lax.conv_general_dilated(volume, weight, (1, 1, 1), ((1, 1), (1, 1), (1, 1)), dimension_numbers=("NCDHW", "OIDHW", "NCDHW"), preferred_element_type=jnp.float32)
    preact = convolved.reshape(C, NX, NY * NZ) + bias_one[:, None, None]
    return values + step_size * jnp.tanh(preact)


def add_forcing(values, forcing):
    if forcing is None:
        return values
    return values + forcing


def descend(level, points, forcing, kernels, biases):
    intervals = len(points) - 1
    spread = 2 ** level
    step_size = step_base * spread

    def advance_to(point_no, previous, size):
        return advance(previous, kernels[point_no * spread - 1], biases[point_no * spread - 1], size)

    points = list(points)
    if level == LEVELS:
        for point_no in range(1, intervals + 1):
            points[point_no] = add_forcing(advance_to(point_no, points[point_no - 1], step_size), forcing[point_no])
        return points
    for point_no in range(1, intervals + 1, 2):
        points[point_no] = add_forcing(advance_to(point_no, points[point_no - 1], step_size), forcing[point_no])
    coarse_points = [points[0]]
    coarse_forcing = [None]
    for point_no in range(2, intervals + 1, 2):
        residue = add_forcing(advance_to(point_no, points[point_no - 1], step_size), forcing[point_no]) - points[point_no]
        coarse_step = advance_to(point_no, points[point_no - 2], 2 * step_size)
        coarse_points.append(points[point_no])
        coarse_forcing.append(residue + (points[point_no] - coarse_step))
    corrected = descend(level + 1, coarse_points, coarse_forcing, kernels, biases)
    for point_no in range(2, intervals + 1, 2):
        points[point_no] = corrected[point_no // 2]
    for point_no in range(1, intervals + 1, 2):
        points[point_no] = add_forcing(advance_to(point_no, points[point_no - 1], step_size), forcing[point_no])
    return points


def reference(initial, kernels, biases):
    points = [initial] * (BLOCKS + 1)
    forcing = [None] * (BLOCKS + 1)
    for repeat in range(CYCLES):
        points = descend(0, points, forcing, kernels, biases)
    return jnp.stack(points[1:])
```

```python
import functools

import jax
import jax.numpy as jnp
from jax import lax
from jax.experimental import pallas as pl
from jax.experimental.pallas import tpu as pltpu
from jax.sharding import PartitionSpec as P

NZ = 64
CYCLES = 2
STEP = 0.125
MESH = pl.DeviceIdType.MESH

W1, W2, W4, U0, U1 = range(5)
DISTANCE = (1, 2, 4, 1, 2)
SOURCE = (2, 2, 2, 0, 1)


def kernel(
    layers,
    slabs,
    init_ref,
    ker_ref,
    bias_ref,
    out_ref,
    weights,
    bias_col,
    init_hi,
    init_f,
    point_hi,
    point_f,
    run,
    t_init,
    t_near,
    t_last,
    msg_hi,
    msg_lo,
    out_hi,
    out_lo,
    gather_send,
    gather_recv,
    send_hi,
    send_lo,
    recv_hi,
    recv_lo,
):
    chans, cells = init_ref.shape
    body_rows = slabs * chans
    rank = lax.axis_index("layer")
    slab = lax.axis_index("space")
    is_even = rank % 2 == 0
    is_first = rank % 4 == 1
    is_coarse = rank % 4 == 3
    depth = jnp.where(is_even, 0, jnp.where(is_first, 1, 2))
    reach = jnp.where(is_even, 1, jnp.where(is_first, 2, 4))

    barrier = pltpu.get_barrier_semaphore()
    for off in range(1, slabs):
        pl.semaphore_signal(
            barrier,
            inc=1,
            device_id=(rank, (slab + off) % slabs),
            device_id_type=MESH,
        )
    pairs = ((1, True, True), (2, rank % 2 == 1, rank % 2 == 1), (4, is_coarse, is_coarse))
    expected = slabs - 1
    for dist, ok_up, ok_down in pairs:
        up = jnp.logical_and(ok_up, rank + dist < layers)
        down = jnp.logical_and(ok_down, rank - dist >= 0)

        @pl.when(up)
        def _():
            pl.semaphore_signal(
                barrier, inc=1, device_id=(rank + dist, slab), device_id_type=MESH
            )

        @pl.when(down)
        def _():
            pl.semaphore_signal(
                barrier, inc=1, device_id=(rank - dist, slab), device_id_type=MESH
            )

        expected = expected + jnp.where(up, 1, 0) + jnp.where(down, 1, 0)

    own_rows = pl.ds(pl.multiple_of((slab + 1) * chans, chans), chans)
    init_hi[own_rows, :] = init_ref[...].astype(jnp.bfloat16)
    pl.semaphore_wait(barrier, expected)

    def gather_copy(off):
        return pltpu.make_async_remote_copy(
            src_ref=init_hi.at[own_rows, :],
            dst_ref=init_hi.at[own_rows, :],
            send_sem=gather_send.at[off],
            recv_sem=gather_recv.at[off],
            device_id=(rank, (slab + off) % slabs),
            device_id_type=MESH,
        )

    for off in range(1, slabs):
        gather_copy(off).start()

    for which in range(2):
        for be in range(9):
            weights[which, be * chans : (be + 1) * chans, :] = jnp.concatenate(
                [ker_ref[which, a * 9 + be] for a in range(3)], axis=1
            )
        rows = lax.broadcasted_iota(jnp.int32, (chans, chans), 0)
        cols = lax.broadcasted_iota(jnp.int32, (chans, chans), 1)
        spread = jnp.where(rows == cols, bias_ref[which : which + 1, :], 0.0)
        bias_col[which] = jnp.broadcast_to(jnp.sum(spread, axis=1, keepdims=True), (chans, 128))
    empty = jnp.zeros((chans, cells), jnp.bfloat16)
    for buf in (init_hi, point_hi):
        buf[0:chans, :] = empty
        buf[body_rows + chans : body_rows + 2 * chans, :] = empty
    for cyc in range(CYCLES):
        for kind in range(5):
            msg_hi[cyc, kind, 0:chans, :] = empty
            msg_hi[cyc, kind, body_rows + chans : body_rows + 2 * chans, :] = empty

    column = lax.broadcasted_iota(jnp.int32, (chans, cells), 1)
    in_z = column % NZ

    def bent(view, which, p):
        window = view[pl.ds(pl.multiple_of(p * chans, chans), 3 * chans), :]
        parts = jnp.dot(weights[which], window, preferred_element_type=jnp.float32)
        total = None
        for e in range(3):
            q = [parts[(3 * b + e) * chans : (3 * b + e + 1) * chans] for b in range(3)]
            lined = (
                q[1]
                + jnp.where(column >= NZ, pltpu.roll(q[0], NZ, 1), 0.0)
                + jnp.where(column < cells - NZ, pltpu.roll(q[2], cells - NZ, 1), 0.0)
            )
            if e == 0:
                lined = jnp.where(in_z > 0, pltpu.roll(lined, 1, 1), 0.0)
            if e == 2:
                lined = jnp.where(in_z < NZ - 1, pltpu.roll(lined, cells - 1, 1), 0.0)
            total = lined if total is None else total + lined
        return jnp.tanh(total + bias_col[which][:, 0:1])

    def plane(view, p):
        return view[pl.ds(pl.multiple_of((p + 1) * chans, chans), chans), :]

    def held(cyc, kind, p):
        low = jnp.where(p == slab, msg_lo[cyc, kind].astype(jnp.float32), 0.0)
        return plane(msg_hi.at[cyc, kind], p).astype(jnp.float32) + low

    def copies(cyc, kind):
        target = (rank + DISTANCE[kind], slab)
        src = SOURCE[kind]
        high = pltpu.make_async_remote_copy(
            src_ref=out_hi.at[cyc, src],
            dst_ref=msg_hi.at[cyc, kind, pl.ds(chans, body_rows), :],
            send_sem=send_hi.at[cyc, kind],
            recv_sem=recv_hi.at[cyc, kind],
            device_id=target,
            device_id_type=MESH,
        )
        low = pltpu.make_async_remote_copy(
            src_ref=out_lo.at[cyc, src],
            dst_ref=msg_lo.at[cyc, kind],
            send_sem=send_lo.at[cyc, kind],
            recv_sem=recv_lo.at[cyc, kind],
            device_id=target,
            device_id_type=MESH,
        )
        return high, low

    def sends(cyc, kind):
        final = cyc == CYCLES - 1
        fits = rank + DISTANCE[kind] < layers
        if kind == W1:
            return fits
        if kind == W2:
            return jnp.logical_and(fits, is_coarse if final else rank % 2 == 1)
        if kind == W4:
            return jnp.logical_and(fits, is_coarse)
        if kind == U0:
            return jnp.logical_and(fits, is_even)
        return jnp.logical_and(fits, is_first)

    def send(cyc, kind):
        @pl.when(sends(cyc, kind))
        def _():
            for copy in copies(cyc, kind):
                copy.start()

    def arrive(cyc, kind):
        for copy in copies(cyc, kind):
            copy.wait_recv()

    def publish(cyc, src, p, value):
        high = value.astype(jnp.bfloat16)
        out_hi[cyc, src, pl.ds(pl.multiple_of(p * chans, chans), chans), :] = high

        @pl.when(p == slab)
        def _():
            out_lo[cyc, src] = (value - high.astype(jnp.float32)).astype(jnp.bfloat16)

    def each_plane(step):
        def body(p, carry):
            step(p)
            return carry

        lax.fori_loop(0, slabs, body, 0)

    def publish_all(cyc, src):
        each_plane(lambda p: publish(cyc, src, p, run[p]))

    for off in range(1, slabs):
        gather_copy(off).wait_recv()

    def spread_init(p):
        init_f[p] = plane(init_hi, p).astype(jnp.float32)

        @pl.when(p == slab)
        def _():
            init_f[p] = init_ref[...]

    each_plane(spread_init)

    for cyc in range(CYCLES):
        if cyc == 0:

            def odd_step(p):
                value = init_f[p] + STEP * bent(init_hi, 0, p)
                point_f[p] = value
                point_hi[pl.ds(pl.multiple_of((p + 1) * chans, chans), chans), :] = value.astype(
                    jnp.bfloat16
                )

            each_plane(odd_step)
        else:

            @pl.when(jnp.logical_and(rank > 0, depth > 0))
            def _():
                arrive(cyc - 1, W1)

            @pl.when(rank > 0)
            def _():
                near = msg_hi.at[cyc - 1, W1]

                def odd_step(p):
                    value = held(cyc - 1, W1, p) + STEP * bent(near, 0, p)
                    point_f[p] = value
                    point_hi[
                        pl.ds(pl.multiple_of((p + 1) * chans, chans), chans), :
                    ] = value.astype(jnp.bfloat16)

                each_plane(odd_step)

        def even_step(p):
            value = point_f[p] + STEP * bent(point_hi, 1, p)
            run[p] = value
            publish(cyc, 0, p, value)

        each_plane(even_step)
        send(cyc, U0)
        if cyc == 0:

            def base_step(p):
                t_init[p] = bent(init_hi, 1, p)

            each_plane(base_step)
        else:

            @pl.when(depth > 0)
            def _():
                def near_step(p):
                    t_near[p] = bent(msg_hi.at[cyc - 1, W1], 1, p)

                each_plane(near_step)

        @pl.when(rank % 2 == 1)
        def _():
            arrive(cyc, U0)

            def step(p):
                fresh = bent(msg_hi.at[cyc, U0], 1, p)
                if cyc == 0:
                    old, t_old = init_f[p], t_init[p]
                else:
                    old, t_old = held(cyc - 1, W1, p), t_near[p]
                value = run[p] + (held(cyc, U0, p) - old) + 2 * STEP * (fresh - t_old)
                run[p] = value
                publish(cyc, 1, p, value)

            each_plane(step)

        send(cyc, U1)

        @pl.when(is_coarse)
        def _():
            if cyc > 0:
                arrive(cyc - 1, W2)

                def near_step(p):
                    t_near[p] = bent(msg_hi.at[cyc - 1, W2], 1, p)

                each_plane(near_step)
            arrive(cyc, U1)

            def step(p):
                fresh = bent(msg_hi.at[cyc, U1], 1, p)
                if cyc == 0:
                    old, t_old = init_f[p], t_init[p]
                else:
                    old, t_old = held(cyc - 1, W2, p), t_near[p]
                run[p] = run[p] + (held(cyc, U1, p) - old) + 4 * STEP * (fresh - t_old)

            each_plane(step)

        @pl.when(rank >= reach)
        def _():
            for kind in (W1, W2, W4):

                @pl.when(depth == kind)
                def _():
                    arrive(cyc, kind)

            size = jnp.where(is_even, 2 * STEP, jnp.where(is_first, 4 * STEP, 8 * STEP))

            def step(p):
                fresh = bent(msg_hi.at[cyc, depth], 1, p)
                if cyc == 0:
                    old, t_old = init_f[p], t_init[p]
                else:
                    old, t_old = held(cyc - 1, depth, p), t_last[p]
                value = run[p] + (held(cyc, depth, p) - old) + size * (fresh - t_old)
                run[p] = value
                if cyc < CYCLES - 1:
                    t_last[p] = fresh

            each_plane(step)

        publish_all(cyc, 2)
        send(cyc, W2)
        send(cyc, W1)
        send(cyc, W4)

    last = CYCLES - 1
    out_ref[1] = run[slab]

    @pl.when(rank == 0)
    def _():
        out_ref[0] = point_f[slab]

    @pl.when(rank > 0)
    def _():
        @pl.when(depth > 0)
        def _():
            arrive(last, W1)

        out_ref[0] = held(last, W1, slab) + STEP * bent(msg_hi.at[last, W1], 0, slab)

    for off in range(1, slabs):
        gather_copy(off).wait_send()
    for cyc in range(CYCLES):
        for kind in range(5):

            @pl.when(sends(cyc, kind))
            def _():
                for copy in copies(cyc, kind):
                    copy.wait_send()


def on_device(initial, kernels, biases):
    layers = lax.axis_size("layer")
    slabs = lax.axis_size("space")
    chans, _, cells = initial.shape
    rows = (slabs + 2) * chans
    f32, b16 = jnp.float32, jnp.bfloat16
    field = pltpu.VMEM((slabs, chans, cells), f32)
    out = pl.pallas_call(
        functools.partial(kernel, layers, slabs),
        out_shape=jax.ShapeDtypeStruct((2, chans, cells), f32),
        in_specs=[pl.BlockSpec(memory_space=pltpu.VMEM)] * 3,
        out_specs=pl.BlockSpec(memory_space=pltpu.VMEM),
        scratch_shapes=[
            pltpu.VMEM((2, 9 * chans, 3 * chans), b16),
            pltpu.VMEM((2, chans, 128), f32),
            pltpu.VMEM((rows, cells), b16),
            field,
            pltpu.VMEM((rows, cells), b16),
            field,
            field,
            field,
            field,
            field,
            pltpu.VMEM((CYCLES, 5, rows, cells), b16),
            pltpu.VMEM((CYCLES, 5, chans, cells), b16),
            pltpu.VMEM((CYCLES, 3, slabs * chans, cells), b16),
            pltpu.VMEM((CYCLES, 3, chans, cells), b16),
            pltpu.SemaphoreType.DMA((slabs,)),
            pltpu.SemaphoreType.DMA((slabs,)),
            pltpu.SemaphoreType.DMA((CYCLES, 5)),
            pltpu.SemaphoreType.DMA((CYCLES, 5)),
            pltpu.SemaphoreType.DMA((CYCLES, 5)),
            pltpu.SemaphoreType.DMA((CYCLES, 5)),
        ],
        compiler_params=pltpu.CompilerParams(
            collective_id=0, has_side_effects=True, vmem_limit_bytes=60 * 1024 * 1024
        ),
    )(initial.reshape(chans, cells), kernels, biases)
    return out.reshape(2, chans, 1, cells)


def solution(mesh):
    return jax.shard_map(
        on_device,
        mesh=mesh,
        in_specs=(P(None, "space", None), P("layer", None, None, None), P("layer", None)),
        out_specs=P("layer", None, "space", None),
        check_vma=False,
    )
```

```python
import functools

import jax
import jax.numpy as jnp
from jax import lax
from jax.experimental import pallas as pl
from jax.experimental.pallas import tpu as pltpu
from jax.sharding import PartitionSpec as P

NZ = 64
CYCLES = 2
STEP = 0.125
MESH = pl.DeviceIdType.MESH

W1, W2, W4, U0, U1 = range(5)
DISTANCE = (1, 2, 4, 1, 2)
SOURCE = (2, 2, 2, 0, 1)


def kernel(
    layers,
    slabs,
    init_ref,
    ker_ref,
    bias_ref,
    out_ref,
    weights,
    bias_col,
    init_hi,
    init_f,
    point_f,
    run,
    t_init,
    t_near,
    t_two,
    t_last,
    wide_point,
    wide_msg,
    wide_near,
    msg_hi,
    msg_lo,
    out_hi,
    out_lo,
    gather_send,
    gather_recv,
    send_hi,
    send_lo,
    recv_hi,
    recv_lo,
):
    chans, _, cells = init_ref.shape
    body_rows = slabs * chans
    rank = lax.axis_index("layer")
    slab = lax.axis_index("space")
    is_even = rank % 2 == 0
    is_first = rank % 4 == 1
    is_coarse = rank % 4 == 3
    depth = jnp.where(is_even, 0, jnp.where(is_first, 1, 2))
    reach = jnp.where(is_even, 1, jnp.where(is_first, 2, 4))

    barrier = pltpu.get_barrier_semaphore()
    for off in range(1, slabs):
        pl.semaphore_signal(
            barrier,
            inc=1,
            device_id=(rank, (slab + off) % slabs),
            device_id_type=MESH,
        )
    pairs = ((1, True, True), (2, rank % 2 == 1, rank % 2 == 1), (4, is_coarse, is_coarse))
    expected = slabs - 1
    for dist, ok_up, ok_down in pairs:
        up = jnp.logical_and(ok_up, rank + dist < layers)
        down = jnp.logical_and(ok_down, rank - dist >= 0)

        @pl.when(up)
        def _():
            pl.semaphore_signal(
                barrier, inc=1, device_id=(rank + dist, slab), device_id_type=MESH
            )

        @pl.when(down)
        def _():
            pl.semaphore_signal(
                barrier, inc=1, device_id=(rank - dist, slab), device_id_type=MESH
            )

        expected = expected + jnp.where(up, 1, 0) + jnp.where(down, 1, 0)

    own_rows = pl.ds(pl.multiple_of((slab + 1) * chans, chans), chans)
    own_init = init_ref[:, 0, :]
    init_hi[own_rows, :] = own_init.astype(jnp.bfloat16)
    pl.semaphore_wait(barrier, expected)

    def gather_copy(off):
        return pltpu.make_async_remote_copy(
            src_ref=init_hi.at[own_rows, :],
            dst_ref=init_hi.at[own_rows, :],
            send_sem=gather_send.at[off],
            recv_sem=gather_recv.at[off],
            device_id=(rank, (slab + off) % slabs),
            device_id_type=MESH,
        )

    for off in range(1, slabs):
        gather_copy(off).start()

    for which in range(2):
        for b in range(3):
            weights[which, b * chans : (b + 1) * chans, :] = jnp.concatenate(
                [ker_ref[which, 9 * a + 3 * b + e] for a in range(3) for e in range(3)], axis=1
            )
        rows = lax.broadcasted_iota(jnp.int32, (chans, chans), 0)
        cols = lax.broadcasted_iota(jnp.int32, (chans, chans), 1)
        spread = jnp.where(rows == cols, bias_ref[which : which + 1, :], 0.0)
        bias_col[which] = jnp.broadcast_to(jnp.sum(spread, axis=1, keepdims=True), (chans, 128))
    empty = jnp.zeros((3 * chans, cells), jnp.bfloat16)
    wide_rows = 3 * chans
    for buf in (wide_point, wide_msg, wide_near):
        buf[0:wide_rows, :] = empty
        buf[(slabs + 1) * wide_rows : (slabs + 2) * wide_rows, :] = empty

    in_z = lax.broadcasted_iota(jnp.int32, (chans, cells), 1) % NZ
    half = lax.broadcasted_iota(jnp.int32, (chans, 2 * NZ), 1) >= NZ
    tiles = cells // (2 * NZ)

    def widen(wide, p, field):
        field = field.astype(jnp.float32)
        before = jnp.where(in_z > 0, pltpu.roll(field, 1, 1), 0.0)
        after = jnp.where(in_z < NZ - 1, pltpu.roll(field, cells - 1, 1), 0.0)
        for e, part in enumerate((before, field, after)):
            start = pl.multiple_of((p + 1) * wide_rows + e * chans, chans)
            wide[pl.ds(start, chans), :] = part.astype(jnp.bfloat16)

    def bent(wide, which, p):
        window = wide[pl.ds(pl.multiple_of(p * wide_rows, wide_rows), 3 * wide_rows), :]
        parts = jnp.dot(weights[which], window, preferred_element_type=jnp.float32)

        def tile(b, j):
            return parts[b * chans : (b + 1) * chans, j * 2 * NZ : (j + 1) * 2 * NZ]

        cols = []
        for j in range(tiles):
            upper = tile(2, j) + tile(0, j - 1) if j > 0 else tile(2, j)
            lower = tile(0, j) + tile(2, j + 1) if j < tiles - 1 else tile(0, j)
            sides = pltpu.roll(jnp.where(half, upper, lower), NZ, 1)
            cols.append(tile(1, j) + sides)
        return jnp.tanh(jnp.concatenate(cols, axis=1) + bias_col[which][:, 0:1])

    def plane(view, p):
        return view[pl.ds(pl.multiple_of((p + 1) * chans, chans), chans), :]

    def held(cyc, kind, p):
        low = msg_lo[cyc, kind, p].astype(jnp.float32)
        return plane(msg_hi.at[cyc, kind], p).astype(jnp.float32) + low

    def copies(cyc, kind, p, source=0, distance=1):
        target = (rank + distance, slab)
        high = pltpu.make_async_remote_copy(
            src_ref=out_hi.at[cyc, source, pl.ds(pl.multiple_of(p * chans, chans), chans), :],
            dst_ref=msg_hi.at[cyc, kind, pl.ds(pl.multiple_of((p + 1) * chans, chans), chans), :],
            send_sem=send_hi.at[cyc, kind, p],
            recv_sem=recv_hi.at[cyc, kind, p],
            device_id=target,
            device_id_type=MESH,
        )
        low = pltpu.make_async_remote_copy(
            src_ref=out_lo.at[cyc, source],
            dst_ref=msg_lo.at[cyc, kind, slab],
            send_sem=send_lo.at[cyc, kind],
            recv_sem=recv_lo.at[cyc, kind],
            device_id=target,
            device_id_type=MESH,
        )
        return high, low

    def sends(cyc, kind):
        final = cyc == CYCLES - 1
        fits = rank + DISTANCE[kind] < layers
        if kind == W1:
            return fits
        if kind == W2:
            return jnp.logical_and(fits, is_coarse if final else rank % 2 == 1)
        if kind == W4:
            return jnp.logical_and(fits, is_coarse)
        if kind == U0:
            return jnp.logical_and(fits, is_even)
        return jnp.logical_and(fits, is_first)

    def send_plane(cyc, kind, p):
        @pl.when(sends(cyc, kind))
        def _():
            high, low = copies(cyc, kind, p, SOURCE[kind], DISTANCE[kind])
            high.start()

            @pl.when(p == slab)
            def _():
                low.start()

    def arrive(cyc, kind, p):
        high, low = copies(cyc, kind, p)
        high.wait_recv()

        @pl.when(p == slab)
        def _():
            low.wait_recv()

    def publish(cyc, src, p, value):
        high = value.astype(jnp.bfloat16)
        out_hi[cyc, src, pl.ds(pl.multiple_of(p * chans, chans), chans), :] = high

        @pl.when(p == slab)
        def _():
            out_lo[cyc, src] = (value - high.astype(jnp.float32)).astype(jnp.bfloat16)

        if src == 0:
            send_plane(cyc, U0, p)
        if src == 1:
            send_plane(cyc, U1, p)
        if src == 2:
            @pl.when(is_coarse)
            def _():
                send_plane(cyc, W2, p)

            @pl.when(jnp.logical_not(is_coarse))
            def _():
                send_plane(cyc, W1, p)

    def each_plane(step):
        def body(p, carry):
            step(p)
            return carry

        lax.fori_loop(0, slabs, body, 0)

    def staged(load, step):
        def body(p, carry):
            @pl.when(p < slabs)
            def _():
                load(p)

            @pl.when(p > 0)
            def _():
                step(p - 1)

            return carry

        lax.fori_loop(0, slabs + 1, body, 0)

    def receive(cyc, kind, wide):
        def load(p):
            arrive(cyc, kind, p)
            widen(wide, p, plane(msg_hi.at[cyc, kind], p))

        return load

    def clear_low(p):
        @pl.when(p != slab)
        def _():
            for cyc in range(CYCLES):
                for kind in range(5):
                    msg_lo[cyc, kind, p] = empty[:chans]

    each_plane(clear_low)
    for off in range(1, slabs):
        gather_copy(off).wait_recv()

    def load_init(p):
        high = plane(init_hi, p)
        widen(wide_near, p, high)
        init_f[p] = high.astype(jnp.float32)

        @pl.when(p == slab)
        def _():
            init_f[p] = own_init

    def set_point(p, value):
        point_f[p] = value
        widen(wide_point, p, value.astype(jnp.bfloat16))

    last = CYCLES - 1
    for cyc in range(CYCLES):
        if cyc == 0:
            staged(load_init, lambda p: set_point(p, init_f[p] + STEP * bent(wide_near, 0, p)))
        else:

            @pl.when(is_coarse)
            def _():
                def two_step(p):
                    t_two[p] = bent(wide_msg, 1, p)

                staged(receive(cyc - 1, W2, wide_msg), two_step)

            @pl.when(rank > 0)
            def _():
                def load(p):
                    @pl.when(depth > 0)
                    def _():
                        arrive(cyc - 1, W1, p)

                    widen(wide_near, p, plane(msg_hi.at[cyc - 1, W1], p))

                staged(
                    load,
                    lambda p: set_point(
                        p, held(cyc - 1, W1, p) + STEP * bent(wide_near, 0, p)
                    ),
                )

        def even_step(p):
            value = point_f[p] + STEP * bent(wide_point, 1, p)
            run[p] = value
            publish(cyc, 0, p, value)

        each_plane(even_step)
        if cyc == 0:

            def base_step(p):
                t_init[p] = bent(wide_near, 1, p)

            each_plane(base_step)
        else:

            @pl.when(depth > 0)
            def _():
                def near_step(p):
                    t_near[p] = bent(wide_near, 1, p)

                each_plane(near_step)

        @pl.when(rank % 2 == 1)
        def _():
            def step(p):
                fresh = bent(wide_msg, 1, p)
                if cyc == 0:
                    old, t_old = init_f[p], t_init[p]
                else:
                    old, t_old = held(cyc - 1, W1, p), t_near[p]
                value = run[p] + (held(cyc, U0, p) - old) + 2 * STEP * (fresh - t_old)
                run[p] = value
                publish(cyc, 1, p, value)

            staged(receive(cyc, U0, wide_msg), step)

        @pl.when(is_coarse)
        def _():
            def step(p):
                fresh = bent(wide_msg, 1, p)
                if cyc == 0:
                    old, t_old = init_f[p], t_init[p]
                else:
                    old, t_old = held(cyc - 1, W2, p), t_two[p]
                run[p] = run[p] + (held(cyc, U1, p) - old) + 4 * STEP * (fresh - t_old)

            staged(receive(cyc, U1, wide_msg), step)

        @pl.when(rank >= reach)
        def _():
            size = jnp.where(is_even, 2 * STEP, jnp.where(is_first, 4 * STEP, 8 * STEP))

            def step(p):
                fresh = bent(wide_msg, 1, p)
                if cyc == 0:
                    old, t_old = init_f[p], t_init[p]
                else:
                    old, t_old = held(cyc - 1, depth, p), t_last[p]
                value = run[p] + (held(cyc, depth, p) - old) + size * (fresh - t_old)
                run[p] = value
                publish(cyc, 2, p, value)
                if cyc < last:
                    t_last[p] = fresh

            staged(receive(cyc, depth, wide_msg), step)

        @pl.when(rank < reach)
        def _():
            each_plane(lambda p: publish(cyc, 2, p, run[p]))

        @pl.when(is_coarse)
        def _():
            each_plane(lambda p: send_plane(cyc, W1, p))
            each_plane(lambda p: send_plane(cyc, W4, p))

        if cyc < last:

            @pl.when(is_first)
            def _():
                each_plane(lambda p: send_plane(cyc, W2, p))

    out_ref[1, :, 0, :] = run[slab]

    @pl.when(rank == 0)
    def _():
        out_ref[0, :, 0, :] = point_f[slab]

    @pl.when(rank > 0)
    def _():
        def load(p):
            @pl.when(depth > 0)
            def _():
                arrive(last, W1, p)

            widen(wide_msg, p, plane(msg_hi.at[last, W1], p))

        each_plane(load)
        out_ref[0, :, 0, :] = held(last, W1, slab) + STEP * bent(wide_msg, 0, slab)

    for off in range(1, slabs):
        gather_copy(off).wait_send()
    for cyc in range(CYCLES):
        for kind in range(5):

            @pl.when(sends(cyc, kind))
            def _():
                def done(p):
                    high, low = copies(cyc, kind, p, SOURCE[kind], DISTANCE[kind])
                    high.wait_send()

                    @pl.when(p == slab)
                    def _():
                        low.wait_send()

                each_plane(done)


def on_device(initial, kernels, biases):
    layers = lax.axis_size("layer")
    slabs = lax.axis_size("space")
    chans, _, cells = initial.shape
    rows = (slabs + 2) * chans
    f32, b16 = jnp.float32, jnp.bfloat16
    field = pltpu.VMEM((slabs, chans, cells), f32)
    return pl.pallas_call(
        functools.partial(kernel, layers, slabs),
        out_shape=jax.ShapeDtypeStruct((2, chans, 1, cells), f32),
        in_specs=[pl.BlockSpec(memory_space=pltpu.VMEM)] * 3,
        out_specs=pl.BlockSpec(memory_space=pltpu.VMEM),
        scratch_shapes=[
            pltpu.VMEM((2, 3 * chans, 9 * chans), b16),
            pltpu.VMEM((2, chans, 128), f32),
            pltpu.VMEM((rows, cells), b16),
            field,
            field,
            field,
            field,
            field,
            field,
            field,
            pltpu.VMEM((3 * rows, cells), b16),
            pltpu.VMEM((3 * rows, cells), b16),
            pltpu.VMEM((3 * rows, cells), b16),
            pltpu.VMEM((CYCLES, 5, rows, cells), b16),
            pltpu.VMEM((CYCLES, 5, slabs, chans, cells), b16),
            pltpu.VMEM((CYCLES, 3, slabs * chans, cells), b16),
            pltpu.VMEM((CYCLES, 3, chans, cells), b16),
            pltpu.SemaphoreType.DMA((slabs,)),
            pltpu.SemaphoreType.DMA((slabs,)),
            pltpu.SemaphoreType.DMA((CYCLES, 5, slabs)),
            pltpu.SemaphoreType.DMA((CYCLES, 5)),
            pltpu.SemaphoreType.DMA((CYCLES, 5, slabs)),
            pltpu.SemaphoreType.DMA((CYCLES, 5)),
        ],
        compiler_params=pltpu.CompilerParams(
            collective_id=0, has_side_effects=True, vmem_limit_bytes=60 * 1024 * 1024
        ),
    )(initial, kernels, biases)


def solution(mesh):
    return jax.shard_map(
        on_device,
        mesh=mesh,
        in_specs=(P(None, "space", None), P("layer", None, None, None), P("layer", None)),
        out_specs=P("layer", None, "space", None),
        check_vma=False,
    )
```

```python
import functools

import jax
import jax.numpy as jnp
from jax import lax
from jax.experimental import pallas as pl
from jax.experimental.pallas import tpu as pltpu
from jax.sharding import PartitionSpec as P

NZ = 64
CYCLES = 2
STEP = 0.125
GROUP = 2
UNROLL = 4
MESH = pl.DeviceIdType.MESH

W1, W2, W4, U0, U1 = range(5)
DISTANCE = (1, 2, 4, 1, 2)
SOURCE = (2, 2, 2, 0, 1)


def rows_at(index, size, count=1):
    start = index * size
    return pl.ds(start if isinstance(start, int) else pl.multiple_of(start, size), count * size)


def kernel(
    layers,
    slabs,
    init_ref,
    ker_ref,
    bias_ref,
    out_ref,
    weights,
    bias_col,
    init_hi,
    init_f,
    point_f,
    run,
    t_init,
    t_near,
    t_two,
    t_last,
    wide_point,
    wide_msg,
    wide_near,
    msg_hi,
    msg_lo,
    out_hi,
    out_lo,
    gather_send,
    gather_recv,
    send_hi,
    send_lo,
    recv_hi,
    recv_lo,
):
    chans, _, cells = init_ref.shape
    body_rows = slabs * chans
    rank = lax.axis_index("layer")
    slab = lax.axis_index("space")
    is_even = rank % 2 == 0
    is_first = rank % 4 == 1
    is_coarse = rank % 4 == 3
    depth = jnp.where(is_even, 0, jnp.where(is_first, 1, 2))
    reach = jnp.where(is_even, 1, jnp.where(is_first, 2, 4))

    barrier = pltpu.get_barrier_semaphore()
    for off in range(1, slabs):
        pl.semaphore_signal(
            barrier,
            inc=1,
            device_id=(rank, (slab + off) % slabs),
            device_id_type=MESH,
        )
    pairs = ((1, True, True), (2, rank % 2 == 1, rank % 2 == 1), (4, is_coarse, is_coarse))
    expected = slabs - 1
    for dist, ok_up, ok_down in pairs:
        up = jnp.logical_and(ok_up, rank + dist < layers)
        down = jnp.logical_and(ok_down, rank - dist >= 0)

        @pl.when(up)
        def _():
            pl.semaphore_signal(
                barrier, inc=1, device_id=(rank + dist, slab), device_id_type=MESH
            )

        @pl.when(down)
        def _():
            pl.semaphore_signal(
                barrier, inc=1, device_id=(rank - dist, slab), device_id_type=MESH
            )

        expected = expected + jnp.where(up, 1, 0) + jnp.where(down, 1, 0)

    own_rows = pl.ds(pl.multiple_of((slab + 1) * chans, chans), chans)
    own_init = init_ref[:, 0, :]
    init_hi[own_rows, :] = own_init.astype(jnp.bfloat16)
    pl.semaphore_wait(barrier, expected)

    def gather_copy(off):
        return pltpu.make_async_remote_copy(
            src_ref=init_hi.at[own_rows, :],
            dst_ref=init_hi.at[own_rows, :],
            send_sem=gather_send.at[off],
            recv_sem=gather_recv.at[off],
            device_id=(rank, (slab + off) % slabs),
            device_id_type=MESH,
        )

    for off in range(1, slabs):
        gather_copy(off).start()

    for which in range(2):
        for b in range(3):
            weights[which, b * chans : (b + 1) * chans, :] = jnp.concatenate(
                [ker_ref[which, 9 * a + 3 * b + e] for a in range(3) for e in range(3)], axis=1
            )
        rows = lax.broadcasted_iota(jnp.int32, (chans, chans), 0)
        cols = lax.broadcasted_iota(jnp.int32, (chans, chans), 1)
        spread = jnp.where(rows == cols, bias_ref[which : which + 1, :], 0.0)
        bias_col[which] = jnp.broadcast_to(jnp.sum(spread, axis=1, keepdims=True), (chans, 128))
    empty = jnp.zeros((3 * chans, cells), jnp.bfloat16)
    wide_rows = 3 * chans
    for buf in (wide_point, wide_msg, wide_near):
        buf[0:wide_rows, :] = empty
        buf[(slabs + 1) * wide_rows : (slabs + 2) * wide_rows, :] = empty

    in_z = lax.broadcasted_iota(jnp.int32, (chans, cells), 1) % NZ
    half = lax.broadcasted_iota(jnp.int32, (chans, 2 * NZ), 1) >= NZ
    tiles = cells // (2 * NZ)

    def widen(wide, p, field):
        field = field.astype(jnp.float32)
        before = jnp.where(in_z > 0, pltpu.roll(field, 1, 1), 0.0)
        after = jnp.where(in_z < NZ - 1, pltpu.roll(field, cells - 1, 1), 0.0)
        for e, part in enumerate((before, field, after)):
            wide[rows_at(3 * (p + 1) + e, chans), :] = part.astype(jnp.bfloat16)

    def bent(wide, which, p):
        window = wide[rows_at(p, wide_rows, 3), :]
        parts = jnp.dot(weights[which], window, preferred_element_type=jnp.float32)

        def tile(b, j):
            return parts[b * chans : (b + 1) * chans, j * 2 * NZ : (j + 1) * 2 * NZ]

        cols = []
        for j in range(tiles):
            upper = tile(2, j) + tile(0, j - 1) if j > 0 else tile(2, j)
            lower = tile(0, j) + tile(2, j + 1) if j < tiles - 1 else tile(0, j)
            sides = pltpu.roll(jnp.where(half, upper, lower), NZ, 1)
            cols.append(tile(1, j) + sides)
        return jnp.tanh(jnp.concatenate(cols, axis=1) + bias_col[which][:, 0:1])

    def plane(view, p):
        return view[rows_at(p + 1, chans), :]

    def held(cyc, kind, p):
        low = msg_lo[cyc, kind, p].astype(jnp.float32)
        return plane(msg_hi.at[cyc, kind], p).astype(jnp.float32) + low

    def copies(cyc, kind, p, source=0, distance=1):
        target = (rank + distance, slab)
        high = pltpu.make_async_remote_copy(
            src_ref=out_hi.at[cyc, source, rows_at(p, chans), :],
            dst_ref=msg_hi.at[cyc, kind, rows_at(p + 1, chans), :],
            send_sem=send_hi.at[cyc, kind, p],
            recv_sem=recv_hi.at[cyc, kind, p],
            device_id=target,
            device_id_type=MESH,
        )
        low = pltpu.make_async_remote_copy(
            src_ref=out_lo.at[cyc, source],
            dst_ref=msg_lo.at[cyc, kind, slab],
            send_sem=send_lo.at[cyc, kind],
            recv_sem=recv_lo.at[cyc, kind],
            device_id=target,
            device_id_type=MESH,
        )
        return high, low

    def sends(cyc, kind):
        final = cyc == CYCLES - 1
        fits = rank + DISTANCE[kind] < layers
        if kind == W1:
            return fits
        if kind == W2:
            return jnp.logical_and(fits, is_coarse if final else rank % 2 == 1)
        if kind == W4:
            return jnp.logical_and(fits, is_coarse)
        if kind == U0:
            return jnp.logical_and(fits, is_even)
        return jnp.logical_and(fits, is_first)

    def send_plane(cyc, kind, p):
        @pl.when(sends(cyc, kind))
        def _():
            high, low = copies(cyc, kind, p, SOURCE[kind], DISTANCE[kind])
            high.start()

            @pl.when(p == slab)
            def _():
                low.start()

    def arrive(cyc, kind, p):
        high, low = copies(cyc, kind, p)
        high.wait_recv()

        @pl.when(p == slab)
        def _():
            low.wait_recv()

    def store(cyc, src, p, value):
        run[p] = value
        out_hi[cyc, src, rows_at(p, chans), :] = value.astype(jnp.bfloat16)

    def publish(cyc, src, p):
        @pl.when(p == slab)
        def _():
            high = out_hi[cyc, src, rows_at(p, chans), :].astype(jnp.float32)
            out_lo[cyc, src] = (run[p] - high).astype(jnp.bfloat16)

        if src == 0:
            send_plane(cyc, U0, p)
        if src == 1:
            send_plane(cyc, U1, p)
        if src == 2:

            @pl.when(is_coarse)
            def _():
                send_plane(cyc, W2, p)

            @pl.when(jnp.logical_not(is_coarse))
            def _():
                send_plane(cyc, W1, p)

    def loop(first, end, step):
        def body(p, carry):
            step(p)
            return carry

        lax.fori_loop(first, end, body, 0)

    def each_plane(step):
        loop(0, slabs, step)

    def grouped(step, after=None, wait=None, prepare=None, group=GROUP):
        if slabs > UNROLL:
            if wait is not None:
                each_plane(wait)
            if prepare is not None:
                each_plane(prepare)
            each_plane(step)
            if after is not None:
                each_plane(after)
            return
        done = prepared = 0
        for p in range(slabs):
            if wait is not None:
                wait(p)
            ready = p if p < slabs - 1 else slabs
            if ready - done >= group or p == slabs - 1:
                if prepare is not None:
                    for q in range(prepared, p + 1):
                        prepare(q)
                for q in range(done, ready):
                    step(q)
                if after is not None:
                    for q in range(done, ready):
                        after(q)
                done, prepared = ready, p + 1

    def received(cyc, kind, wide, step, after=None, guard=None):
        def wait(p):
            if guard is None:
                arrive(cyc, kind, p)
            else:

                @pl.when(guard)
                def _():
                    arrive(cyc, kind, p)

        grouped(step, after, wait, lambda p: widen(wide, p, plane(msg_hi.at[cyc, kind], p)))

    def clear_low(p):
        @pl.when(p != slab)
        def _():
            for cyc in range(CYCLES):
                for kind in range(5):
                    msg_lo[cyc, kind, p] = empty[:chans]

    each_plane(clear_low)
    for off in range(1, slabs):
        gather_copy(off).wait_recv()

    init_f[slab] = own_init

    def copy_init(p):
        @pl.when(p != slab)
        def _():
            init_f[p] = plane(init_hi, p).astype(jnp.float32)

    each_plane(copy_init)

    def set_point(p, value):
        point_f[p] = value
        widen(wide_point, p, value.astype(jnp.bfloat16))

    last = CYCLES - 1
    for cyc in range(CYCLES):
        if cyc == 0:
            grouped(
                lambda p: set_point(p, init_f[p] + STEP * bent(wide_near, 0, p)),
                prepare=lambda p: widen(wide_near, p, plane(init_hi, p)),
                group=slabs,
            )
        else:

            @pl.when(is_coarse)
            def _():
                def two_step(p):
                    t_two[p] = bent(wide_msg, 1, p)

                received(cyc - 1, W2, wide_msg, two_step)

            @pl.when(rank > 0)
            def _():
                received(
                    cyc - 1,
                    W1,
                    wide_near,
                    lambda p: set_point(
                        p, held(cyc - 1, W1, p) + STEP * bent(wide_near, 0, p)
                    ),
                    guard=depth > 0,
                )

        def even_step(p):
            store(cyc, 0, p, point_f[p] + STEP * bent(wide_point, 1, p))

        grouped(even_step, lambda p: publish(cyc, 0, p))
        if cyc == 0:

            def base_step(p):
                t_init[p] = bent(wide_near, 1, p)

            grouped(base_step, group=slabs)
        else:

            @pl.when(depth > 0)
            def _():
                def near_step(p):
                    t_near[p] = bent(wide_near, 1, p)

                grouped(near_step, group=slabs)

        @pl.when(rank % 2 == 1)
        def _():
            def step(p):
                fresh = bent(wide_msg, 1, p)
                if cyc == 0:
                    old, t_old = init_f[p], t_init[p]
                else:
                    old, t_old = held(cyc - 1, W1, p), t_near[p]
                value = run[p] + (held(cyc, U0, p) - old) + 2 * STEP * (fresh - t_old)
                store(cyc, 1, p, value)

            received(cyc, U0, wide_msg, step, lambda p: publish(cyc, 1, p))

        @pl.when(is_coarse)
        def _():
            def step(p):
                fresh = bent(wide_msg, 1, p)
                if cyc == 0:
                    old, t_old = init_f[p], t_init[p]
                else:
                    old, t_old = held(cyc - 1, W2, p), t_two[p]
                run[p] = run[p] + (held(cyc, U1, p) - old) + 4 * STEP * (fresh - t_old)

            received(cyc, U1, wide_msg, step)

        @pl.when(rank >= reach)
        def _():
            size = jnp.where(is_even, 2 * STEP, jnp.where(is_first, 4 * STEP, 8 * STEP))

            def step(p):
                fresh = bent(wide_msg, 1, p)
                if cyc == 0:
                    old, t_old = init_f[p], t_init[p]
                else:
                    old, t_old = held(cyc - 1, depth, p), t_last[p]
                value = run[p] + (held(cyc, depth, p) - old) + size * (fresh - t_old)
                store(cyc, 2, p, value)
                if cyc < last:
                    t_last[p] = fresh

            received(cyc, depth, wide_msg, step, lambda p: publish(cyc, 2, p))

        @pl.when(rank < reach)
        def _():
            def keep(p):
                store(cyc, 2, p, run[p])
                publish(cyc, 2, p)

            each_plane(keep)

        @pl.when(is_coarse)
        def _():
            each_plane(lambda p: send_plane(cyc, W1, p))
            each_plane(lambda p: send_plane(cyc, W4, p))

        if cyc < last:

            @pl.when(is_first)
            def _():
                each_plane(lambda p: send_plane(cyc, W2, p))

    out_ref[1, :, 0, :] = run[slab]

    @pl.when(rank == 0)
    def _():
        out_ref[0, :, 0, :] = point_f[slab]

    @pl.when(rank > 0)
    def _():
        def load(p):
            @pl.when(depth > 0)
            def _():
                arrive(last, W1, p)

            widen(wide_msg, p, plane(msg_hi.at[last, W1], p))

        each_plane(load)
        out_ref[0, :, 0, :] = held(last, W1, slab) + STEP * bent(wide_msg, 0, slab)

    for off in range(1, slabs):
        gather_copy(off).wait_send()
    for cyc in range(CYCLES):
        for kind in range(5):

            @pl.when(sends(cyc, kind))
            def _():
                def done(p):
                    high, low = copies(cyc, kind, p, SOURCE[kind], DISTANCE[kind])
                    high.wait_send()

                    @pl.when(p == slab)
                    def _():
                        low.wait_send()

                each_plane(done)


def on_device(initial, kernels, biases):
    layers = lax.axis_size("layer")
    slabs = lax.axis_size("space")
    chans, _, cells = initial.shape
    rows = (slabs + 2) * chans
    f32, b16 = jnp.float32, jnp.bfloat16
    field = pltpu.VMEM((slabs, chans, cells), f32)
    return pl.pallas_call(
        functools.partial(kernel, layers, slabs),
        out_shape=jax.ShapeDtypeStruct((2, chans, 1, cells), f32),
        in_specs=[pl.BlockSpec(memory_space=pltpu.VMEM)] * 3,
        out_specs=pl.BlockSpec(memory_space=pltpu.VMEM),
        scratch_shapes=[
            pltpu.VMEM((2, 3 * chans, 9 * chans), b16),
            pltpu.VMEM((2, chans, 128), f32),
            pltpu.VMEM((rows, cells), b16),
            field,
            field,
            field,
            field,
            field,
            field,
            field,
            pltpu.VMEM((3 * rows, cells), b16),
            pltpu.VMEM((3 * rows, cells), b16),
            pltpu.VMEM((3 * rows, cells), b16),
            pltpu.VMEM((CYCLES, 5, rows, cells), b16),
            pltpu.VMEM((CYCLES, 5, slabs, chans, cells), b16),
            pltpu.VMEM((CYCLES, 3, slabs * chans, cells), b16),
            pltpu.VMEM((CYCLES, 3, chans, cells), b16),
            pltpu.SemaphoreType.DMA((slabs,)),
            pltpu.SemaphoreType.DMA((slabs,)),
            pltpu.SemaphoreType.DMA((CYCLES, 5, slabs)),
            pltpu.SemaphoreType.DMA((CYCLES, 5)),
            pltpu.SemaphoreType.DMA((CYCLES, 5, slabs)),
            pltpu.SemaphoreType.DMA((CYCLES, 5)),
        ],
        compiler_params=pltpu.CompilerParams(
            collective_id=0, has_side_effects=True, vmem_limit_bytes=60 * 1024 * 1024
        ),
    )(initial, kernels, biases)


def solution(mesh):
    return jax.shard_map(
        on_device,
        mesh=mesh,
        in_specs=(P(None, "space", None), P("layer", None, None, None), P("layer", None)),
        out_specs=P("layer", None, "space", None),
        check_vma=False,
    )
```
